256 devices in a mesh: aux: 8 (over x, core), orb: 32 (over z, y).
Axes of the slice: x: 4, y: 4, z: 8, core: 2. Of those that a mesh axis runs over, the one named last changes fastest.
Arguments:
- three_center: float32 [32, 32, 128, 1024], P('aux', 'orb'), may hold values from -6 to 6
- tile_lists: int32 [2, 32, 8, 8], P(None, 'aux'), may hold values from -1 to 7, as said below
- occ_density: float32 [2, 1024, 1024], P(None, 'orb', 'aux'), may hold values from -0.1875 to 0.1875
- vir_density: float32 [2, 1024, 1024], P(None, 'orb', 'aux'), may hold values from -0.1875 to 0.1875
Outputs:
- coupled: float32 [2, 32, 32, 1024, 128], P(None, 'aux', 'orb')
The draws below stay inside these ranges and needn't reach their ends.
Inputs may be any that keep to these rules, and one draw needn't show every extreme that they name: Row m of tile_lists[t, j] names distinct orbital blocks in rising order, block m always among them, and -1 in the remaining places; it names between 2 and 8 blocks, and for every t and j one row names all 8 and another exactly 2.
All inputs are finite; a program needn't handle non-finite values.
Results may differ from the reference program's by a relative error of at most 0.0003.
Values sent between devices are 32-bit elements; how exact they have to be, the bound alone decides.
A program may use at most 64 MiB of HBM per device.

```python
import jax
import jax.numpy as jnp
from jax import lax

ORB = 1024
BLK = 128
AUX_Q = 4
TIMES = 2
NB = 8
ABLOCKS = 32
AUX_ROWS = 32
N_AUX = 8
N_ORB = 32


def draw_tile_lists(key, part):
    group_total = TIMES * ABLOCKS
    row_total = group_total * NB
    base = jax.random.fold_in(key, 7)
    key_count, key_full, key_low, key_score = jax.random.split(base, 4)
    counts = jax.random.randint(key_count, (row_total,), 2, NB + 1)
    full_pick = jax.random.randint(key_full, (group_total,), 0, NB)
    low_pick = (full_pick + 1 + jax.random.randint(key_low, (group_total,), 0, NB - 1)) % NB
    positions = jnp.arange(row_total, dtype=jnp.int32)
    within = positions % NB
    group_ids = positions // NB
    counts = jnp.where(within == full_pick[group_ids], NB, counts)
    counts = jnp.where(within == low_pick[group_ids], 2, counts)
    block_ids = jnp.arange(NB, dtype=jnp.int32)
    scores = jax.random.randint(key_score, (row_total, NB), 0, 1048576) * NB + block_ids[None, :]
    scores = jnp.where(block_ids[None, :] == within[:, None], -1, scores)
    ordering = jnp.argsort(scores, axis=1, stable=True)
    ranking = jnp.argsort(ordering, axis=1, stable=True)
    chosen = ranking < counts[:, None]
    sort_key = jnp.where(chosen, block_ids[None, :], NB + block_ids[None, :])
    listed = jnp.sort(sort_key, axis=1)
    listed = jnp.where(listed < NB, listed, -1)
    return listed.reshape(TIMES, ABLOCKS, NB, NB).astype(jnp.int32)


def steps_of(rng, dims, shards, smallest, top_value):
    factor_of = 1.0
    for axis_at, parts in shards:
        draws = jax.random.uniform(jax.random.fold_in(jax.random.fold_in(rng, 6), axis_at), (parts,), jnp.float32, smallest / len(shards), top_value / len(shards))
        factor_of = factor_of * jnp.repeat(jnp.exp(draws), dims[axis_at] // parts).reshape((-1,) + (1,) * (len(dims) - 1 - axis_at))
    return factor_of


def gaussian(rng, dims, spread, limit, cuts=(), kind=jnp.bfloat16):
    array = spread * jax.random.normal(rng, dims, jnp.float32)
    if cuts:
        array = array * steps_of(rng, dims, cuts, -0.22, 0.18)
    return jnp.clip(array, -limit, limit).astype(kind)


def setup_inputs(seed: int = 0) -> dict:
    splits = jax.random.split(jax.random.key(seed), 5)
    return {
        "three_center": gaussian(splits[0], (AUX_ROWS, N_ORB, BLK, ORB), 1.0, 6.0, ((0, 8), (1, 32)), jnp.float32),
        "tile_lists": draw_tile_lists(jax.random.fold_in(splits[4], 71), 0),
        "occ_density": gaussian(splits[2], (TIMES, ORB, ORB), ORB ** -0.5, 0.1875, ((1, 32), (2, 8)), jnp.float32),
        "vir_density": gaussian(splits[3], (TIMES, ORB, ORB), ORB ** -0.5, 0.1875, ((1, 32), (2, 8)), jnp.float32),
    }


def reference(three_center, tile_lists, occ_density, vir_density):
    block_count = ORB // BLK
    split_count = N_ORB // block_count
    aux_share = AUX_Q // split_count
    grouped = three_center.reshape(N_AUX, AUX_Q, block_count, split_count, BLK, ORB)
    block_ids = jnp.arange(block_count, dtype=jnp.int32)
    outputs = []
    for moment in range(TIMES):
        occ_now = occ_density[moment]
        vir_now = vir_density[moment]

        def per_block(inputs):
            block_number, listed_rows = inputs
            column = block_number // split_count
            part_number = block_number % split_count
            chosen = lax.dynamic_index_in_dim(grouped, column, 0, keepdims=False)
            chosen = lax.dynamic_index_in_dim(chosen, part_number, 2, keepdims=False)
            integrals = chosen.reshape(AUX_Q, ORB, ORB)
            matches = listed_rows[:, :, None] == block_ids[None, None, :]
            listed = jnp.sum(matches.astype(jnp.float32), axis=1)
            tile_keep = jnp.repeat(jnp.repeat(listed, BLK, axis=0), BLK, axis=1)
            masked = integrals * tile_keep[None]
            half = jnp.dot(masked.reshape(AUX_Q * ORB, ORB), occ_now,
                           precision=lax.Precision.HIGHEST,
                           preferred_element_type=jnp.float32).reshape(AUX_Q, ORB, ORB)
            half = half * tile_keep[None]
            full = jnp.einsum("sk,akl->asl", vir_now, half, precision=lax.Precision.HIGHEST)
            arranged = full.reshape(split_count, aux_share, ORB, block_count, BLK)
            arranged = arranged.transpose(1, 3, 0, 2, 4)
            return arranged.reshape(aux_share, N_ORB, ORB, BLK)

        block_numbers = jnp.arange(N_AUX * split_count, dtype=jnp.int32)
        blocks = lax.map(per_block, (block_numbers, tile_lists[moment]))
        outputs.append(blocks.reshape(N_AUX * AUX_Q, N_ORB, ORB, BLK))
    return jnp.stack(outputs, axis=0)
```

```python
import functools

import jax
import jax.numpy as jnp
from jax import lax
from jax.experimental import pallas as pl
from jax.experimental.pallas import tpu as pltpu
from jax.sharding import PartitionSpec as P

MESH = pl.DeviceIdType.MESH
NX, NC, NZ, NY = 4, 2, 8, 4
BLK = 128
OCC, VIR = 0, 1


def listed_mask(tile_lists, part_index, block_index):
    block_table = lax.dynamic_index_in_dim(tile_lists, part_index, 1, keepdims=False)
    listed_row = lax.dynamic_index_in_dim(block_table, block_index, 1, keepdims=False)
    block_count = tile_lists.shape[3]
    block_ids = jnp.arange(block_count, dtype=jnp.int32)
    matches = listed_row[:, :, None] == block_ids[None, None, :]
    return jnp.sum(matches.astype(jnp.float32), axis=1)


def split(value):
    high = value.astype(jnp.bfloat16)
    return high, (value - high.astype(jnp.float32)).astype(jnp.bfloat16)


def three_pass(a_high, a_low, b_high, b_low):
    dot = functools.partial(jnp.dot, preferred_element_type=jnp.float32)
    return dot(a_high, b_high) + dot(a_high, b_low) + dot(a_low, b_high)


def kernel(
    mask, three_center, occ_in, vir_in, coupled,
    rows, int_high, int_low, occ, vir, sending, received,
    one_high, one_low, two_high, two_low,
    rows_sem, own_sem, zs, zr, ys, yr, xs, xr, rs, rr, cs, cr, out_sem, in_sem,
):
    aux, orb = lax.axis_index("aux"), lax.axis_index("orb")
    x, c, z, y = lax.div(aux, NC), lax.rem(aux, NC), lax.div(orb, NY), lax.rem(orb, NY)
    pair = lax.div(z, 2)
    inputs, full = (occ_in, vir_in), (occ, vir)

    def device(at_x, at_c, at_z, at_y):
        return (at_x * NC + at_c, at_z * NY + at_y)

    def along_x(step):
        return lax.rem(x + step + NX, NX)

    def along_z(step):
        return lax.rem(z + step, NZ)

    def along_y(step):
        return lax.rem(y + step, NY)

    def send(source, target, send_sem, recv_sem, to):
        pltpu.make_async_remote_copy(
            src_ref=source, dst_ref=target, send_sem=send_sem, recv_sem=recv_sem,
            device_id=to, device_id_type=MESH,
        ).start()

    def wait(ref, sem):
        pltpu.make_async_copy(ref, ref, sem).wait()

    def own_copy(g, t):
        return pltpu.make_async_copy(inputs[g].at[t], full[g].at[t, aux, z, y], own_sem.at[g, t])

    rows_copy = pltpu.make_async_copy(three_center.at[:, 0], rows, rows_sem)
    for g in (OCC, VIR):
        for t in range(2):
            own_copy(g, t).start()
    rows_copy.start()

    barrier = pltpu.get_barrier_semaphore()
    peers = [device(x, c, along_z(d), y) for d in range(1, NZ)]
    peers += [device(x, c, z, along_y(d)) for d in range(1, NY)]
    peers += [device(along_x(d), c, z, y) for d in (1, -1)]
    peers += [device(x, 1 - c, z, y)]
    for peer in peers:
        pl.semaphore_signal(barrier, inc=1, device_id=peer, device_id_type=MESH)
    pl.semaphore_wait(barrier, len(peers))

    def z_start(g, t):
        own_copy(g, t).wait()
        piece = full[g].at[t, aux, z, y]
        for d in (4, 3, 5, 2, 6, 1, 7):
            send(piece, piece, zs.at[g, t], zr.at[g, t], device(x, c, along_z(d), y))

    def z_wait(g, t):
        wait(full[g].at[t, aux, pl.ds(0, NZ - 1), y], zr.at[g, t])

    def y_start(g, t):
        piece = full[g].at[t, aux, :, y]
        for d in (2, 1, 3):
            send(piece, piece, ys.at[g, t], yr.at[g, t], device(x, c, z, along_y(d)))

    def y_wait(g, t):
        wait(full[g].at[t, aux, :, pl.ds(0, NY - 1)], yr.at[g, t])

    def column(g, t, at_x):
        return full[g].at[t, at_x * NC + c]

    def core_start(g, t, at_x):
        piece = column(g, t, at_x)
        send(piece, piece, cs.at[g, t], cr.at[g, t], device(x, 1 - c, z, y))

    def core_wait(g, t):
        wait(full[g].at[t, pl.ds(0, NX)], cr.at[g, t])

    def x_start(g, t):
        piece = column(g, t, x)
        send(piece, piece, xs.at[g, t], xr.at[g, t, 0], device(along_x(1), c, z, y))
        send(piece, piece, xs.at[g, t], xr.at[g, t, 1], device(along_x(-1), c, z, y))
        core_start(g, t, x)

    def x_relay(g, t):
        for side, (origin, onward) in enumerate(((-1, 1), (1, -1))):
            at_x = along_x(origin)
            wait(column(g, t, at_x), xr.at[g, t, side])
            piece = full[g].at[t, at_x * NC + c, pl.ds(side * (NZ // 2), NZ // 2)]
            send(piece, piece, rs.at[g, t], rr.at[g, t], device(along_x(onward), c, z, y))
            core_start(g, t, at_x)

    def x_finish(g, t):
        at_x = along_x(2)
        wait(column(g, t, at_x), rr.at[g, t])
        core_start(g, t, at_x)

    def half_stage(t):
        def unit(k, carry):
            p = lax.rem(pair + 2 + k, NX)
            for h in range(2):
                for n in range(NZ):
                    block = occ[t, 2 * p + h, n].reshape(BLK, BLK)
                    block = block * mask[pl.ds(t * NZ + n, 1), :]
                    high, low = split(block)
                    one_high[pl.ds(n * BLK, BLK), pl.ds(h * BLK, BLK)] = high
                    one_low[pl.ds(n * BLK, BLK), pl.ds(h * BLK, BLK)] = low
            product = three_pass(int_high[...], int_low[...], one_high[...], one_low[...])
            for h in range(2):
                keep = mask[pl.ds(t * NZ + 2 * p + h, 1), :]
                for r in range(NY):
                    part = product[r * BLK : (r + 1) * BLK, h * BLK : (h + 1) * BLK]
                    sending[t, 2 * p + h, r] = part * keep
            for h in range(2):
                to_z = 2 * p + h
                for r in range(NY):
                    own = jnp.logical_and(to_z == z, y == r)
                    source = sending.at[t, to_z, r]
                    target = received.at[t, z, y]
                    arrived = in_sem.at[t, pair]

                    @pl.when(own)
                    def _():
                        pltpu.make_async_copy(source, target, arrived).start()

                    @pl.when(jnp.logical_not(own))
                    def _():
                        send(source, target, out_sem.at[t], arrived, device(x, c, to_z, r))

            return carry

        lax.fori_loop(0, NX, unit, 0)

    def full_stage(t):
        def unit(k, carry):
            p = lax.rem(pair + 2 - k + NX, NX)
            wait(received.at[t, pl.ds(2 * p, 2)], in_sem.at[t, p])
            for h in range(2):
                for q in range(NY):
                    high, low = split(received[t, 2 * p + h, q])
                    two_high[pl.ds(h * BLK, BLK), pl.ds(q * BLK, BLK)] = high
                    two_low[pl.ds(h * BLK, BLK), pl.ds(q * BLK, BLK)] = low

            def tile(s, inner):
                halves = [
                    split(vir[t, 2 * p + h, pl.ds(2 * s, 2)].reshape(2 * BLK, BLK))
                    for h in range(2)
                ]
                high = jnp.concatenate([halves[0][0], halves[1][0]], axis=1)
                low = jnp.concatenate([halves[0][1], halves[1][1]], axis=1)
                product = three_pass(high, low, two_high[...], two_low[...])
                for q in range(NY):
                    at = (t, q, pl.ds(s * 2 * BLK, 2 * BLK), slice(None))
                    coupled[at] += product[:, q * BLK : (q + 1) * BLK]
                return inner

            lax.fori_loop(0, NZ // 2, tile, 0)
            return carry

        lax.fori_loop(0, NX, unit, 0)

    z_start(OCC, 0)
    rows_copy.wait()
    for r in range(NY):
        high, low = split(rows[r])
        int_high[pl.ds(r * BLK, BLK), :] = high
        int_low[pl.ds(r * BLK, BLK), :] = low

    z_wait(OCC, 0)
    y_start(OCC, 0)
    z_start(OCC, 1)
    y_wait(OCC, 0)
    x_start(OCC, 0)
    z_wait(OCC, 1)
    y_start(OCC, 1)
    z_start(VIR, 0)
    z_start(VIR, 1)
    coupled[...] = jnp.zeros_like(coupled)
    x_relay(OCC, 0)
    y_wait(OCC, 1)
    x_start(OCC, 1)
    x_finish(OCC, 0)
    z_wait(VIR, 0)
    y_start(VIR, 0)
    z_wait(VIR, 1)
    y_start(VIR, 1)
    core_wait(OCC, 0)
    half_stage(0)
    x_relay(OCC, 1)
    y_wait(VIR, 0)
    x_start(VIR, 0)
    x_finish(OCC, 1)
    core_wait(OCC, 1)
    half_stage(1)
    x_relay(VIR, 0)
    y_wait(VIR, 1)
    x_start(VIR, 1)
    x_finish(VIR, 0)
    core_wait(VIR, 0)
    x_relay(VIR, 1)
    x_finish(VIR, 1)
    core_wait(VIR, 1)
    full_stage(0)
    full_stage(1)

    for g in (OCC, VIR):
        for t in range(2):
            wait(full[g].at[t, aux, pl.ds(0, NZ - 1), y], zs.at[g, t])
            wait(full[g].at[t, aux, :, pl.ds(0, NY - 1)], ys.at[g, t])
            wait(full[g].at[t, pl.ds(0, 2)], xs.at[g, t])
            wait(full[g].at[t, 0], rs.at[g, t])
            wait(full[g].at[t, pl.ds(0, NX)], cs.at[g, t])
    for t in range(2):
        wait(sending.at[t, pl.ds(0, NZ - 1)], out_sem.at[t])
        wait(sending.at[t, 0, pl.ds(0, NY - 1)], out_sem.at[t])


def local(three_center, tile_lists, occ_density, vir_density):
    owner_unit = lax.axis_index("orb")
    listed = listed_mask(tile_lists, owner_unit % NY, owner_unit // NY)
    times, blocks = listed.shape
    mask = jnp.broadcast_to(listed.reshape(times * blocks, 1), (times * blocks, BLK))
    orbitals = three_center.shape[3]
    dma = pltpu.SemaphoreType.DMA
    coupled = pl.pallas_call(
        kernel,
        out_shape=jax.ShapeDtypeStruct((times, NY, orbitals, BLK), jnp.float32),
        in_specs=[pl.BlockSpec(memory_space=pltpu.VMEM)]
        + [pl.BlockSpec(memory_space=pl.ANY)] * 3,
        out_specs=pl.BlockSpec(memory_space=pltpu.VMEM),
        scratch_shapes=[
            pltpu.VMEM((NY, BLK, orbitals), jnp.float32),
            pltpu.VMEM((NY * BLK, orbitals), jnp.bfloat16),
            pltpu.VMEM((NY * BLK, orbitals), jnp.bfloat16),
            pltpu.VMEM((times, NX * NC, NZ, NY, 32, BLK), jnp.float32),
            pltpu.VMEM((times, NX * NC, NZ, NY, 32, BLK), jnp.float32),
            pltpu.VMEM((times, NZ, NY, BLK, BLK), jnp.float32),
            pltpu.VMEM((times, NZ, NY, BLK, BLK), jnp.float32),
            pltpu.VMEM((orbitals, 2 * BLK), jnp.bfloat16),
            pltpu.VMEM((orbitals, 2 * BLK), jnp.bfloat16),
            pltpu.VMEM((2 * BLK, NY * BLK), jnp.bfloat16),
            pltpu.VMEM((2 * BLK, NY * BLK), jnp.bfloat16),
            dma(()),
            dma((2, 2)),
            dma((2, 2)),
            dma((2, 2)),
            dma((2, 2)),
            dma((2, 2)),
            dma((2, 2)),
            dma((2, 2, 2)),
            dma((2, 2)),
            dma((2, 2)),
            dma((2, 2)),
            dma((2, 2)),
            dma((2,)),
            dma((2, NX)),
        ],
        compiler_params=pltpu.CompilerParams(
            collective_id=0, has_side_effects=True, vmem_limit_bytes=60 * 2**20
        ),
        name="contract",
    )(mask, three_center, occ_density, vir_density)
    return coupled[:, :, None]


def solution(mesh):
    in_specs = (
        P("aux", "orb", None, None),
        P(None, "aux", None, None),
        P(None, "orb", "aux"),
        P(None, "orb", "aux"),
    )
    out_specs = P(None, "aux", "orb", None, None)
    return jax.shard_map(local, mesh=mesh, in_specs=in_specs, out_specs=out_specs, check_vma=False)
```

```python
import functools

import jax
import jax.numpy as jnp
from jax import lax
from jax.experimental import pallas as pl
from jax.experimental.pallas import tpu as pltpu
from jax.sharding import PartitionSpec as P

MESH = pl.DeviceIdType.MESH
NX, NC, NZ, NY = 4, 2, 8, 4
BLK = 128
OCC, VIR = 0, 1


def split(value):
    high = value.astype(jnp.bfloat16)
    return high, (value - high.astype(jnp.float32)).astype(jnp.bfloat16)


def three_pass(a_high, a_low, b_high, b_low):
    dot = functools.partial(jnp.dot, preferred_element_type=jnp.float32)
    return dot(a_high, b_high) + dot(a_high, b_low) + dot(a_low, b_high)


def kernel(
    tile_lists, three_center, occ_in, vir_in, coupled,
    lists, mask, rows, int_high, int_low, occ, vir, sending, received,
    one_high, one_low, two_high, two_low,
    rows_sem, own_sem, zs, zr, ys, yr, xs, xr, rs, rr, cs, cr, out_sem, in_sem,
    x0s, x0r, z0s, z0r, y0s, y0r, r0s, r0r, c0s, c0r,
):
    aux, orb = lax.axis_index("aux"), lax.axis_index("orb")
    x, c, z, y = lax.div(aux, NC), lax.rem(aux, NC), lax.div(orb, NY), lax.rem(orb, NY)
    pair = lax.div(z, 2)
    inputs, full = (occ_in, vir_in), (occ, vir)

    def device(at_x, at_c, at_z, at_y):
        return (at_x * NC + at_c, at_z * NY + at_y)

    def along_x(step):
        return lax.rem(x + step + NX, NX)

    def along_z(step):
        return lax.rem(z + step, NZ)

    def along_y(step):
        return lax.rem(y + step, NY)

    def send(source, target, send_sem, recv_sem, to):
        pltpu.make_async_remote_copy(
            src_ref=source, dst_ref=target, send_sem=send_sem, recv_sem=recv_sem,
            device_id=to, device_id_type=MESH,
        ).start()

    def wait(ref, sem):
        pltpu.make_async_copy(ref, ref, sem).wait()

    def own_copy(g, t):
        return pltpu.make_async_copy(inputs[g].at[t], full[g].at[t, x, c, z, y], own_sem.at[g, t])

    rows_copy = pltpu.make_async_copy(three_center.at[:, 0], rows, rows_sem.at[0])
    lists_copy = pltpu.make_async_copy(tile_lists.at[:, y], lists, rows_sem.at[1])
    for g in (OCC, VIR):
        for t in range(2):
            own_copy(g, t).start()
    lists_copy.start()
    rows_copy.start()

    barrier = pltpu.get_barrier_semaphore()
    peers = [device(x, c, along_z(d), y) for d in range(1, NZ)]
    peers += [device(x, c, z, along_y(d)) for d in range(1, NY)]
    peers += [device(along_x(d), c, z, y) for d in range(1, NX)]
    peers += [device(x, 1 - c, z, y)]
    for peer in peers:
        pl.semaphore_signal(barrier, inc=1, device_id=peer, device_id_type=MESH)
    pl.semaphore_wait(barrier, len(peers))

    def wanted(at_z, k):
        return lax.rem(lax.div(at_z, 2) + 2 + k, NX)

    def first_x_start():
        own_copy(OCC, 0).wait()
        piece = occ.at[0, x, c, z, y]
        for d in (2, 1, 3):
            send(piece, piece, x0s, x0r, device(along_x(d), c, z, y))

    def first_z_start():
        wait(occ.at[0, pl.ds(0, NX - 1), c, z, y], x0r)
        for k in range(NX):
            for d in (4, 3, 5, 2, 6, 1, 7):
                at_z = along_z(d)
                piece = occ.at[0, wanted(at_z, k), c, z, y]
                send(piece, piece, z0s, z0r.at[k], device(x, c, at_z, y))

    def first_y_start(k):
        wait(occ.at[0, 0, c, pl.ds(0, NZ - 1), y], z0r.at[k])
        piece = occ.at[0, wanted(z, k), c, :, y]
        for side, step in enumerate((1, 3)):
            send(piece, piece, y0s, y0r.at[k, side], device(x, c, z, along_y(step)))

    def first_y_relay(k):
        for side, (origin, onward) in enumerate(((3, 1), (1, 3))):
            from_y, to_y = along_y(origin), along_y(onward)
            wait(occ.at[0, 0, c, :, from_y], y0r.at[k, side])
            piece = occ.at[0, wanted(z, k), c, pl.ds(side * (NZ // 2), NZ // 2), from_y]
            send(piece, piece, r0s, r0r.at[k], device(x, c, z, to_y))

    def first_finish(k):
        wait(occ.at[0, 0, c, :, y], r0r.at[k])
        piece = occ.at[0, wanted(z, k), c]
        send(piece, piece, c0s, c0r.at[k], device(x, 1 - c, z, y))
        wait(piece, c0r.at[k])

    def z_start(g, t):
        own_copy(g, t).wait()
        piece = full[g].at[t, x, c, z, y]
        for d in (4, 3, 5, 2, 6, 1, 7):
            send(piece, piece, zs.at[g, t], zr.at[g, t], device(x, c, along_z(d), y))

    def z_wait(g, t):
        wait(full[g].at[t, x, c, pl.ds(0, NZ - 1), y], zr.at[g, t])

    def y_start(g, t):
        piece = full[g].at[t, x, c, :, y]
        for d in (2, 1, 3):
            send(piece, piece, ys.at[g, t], yr.at[g, t], device(x, c, z, along_y(d)))

    def y_wait(g, t):
        wait(full[g].at[t, x, c, :, pl.ds(0, NY - 1)], yr.at[g, t])

    def column(g, t, at_x):
        return full[g].at[t, at_x, c]

    def core_start(g, t, at_x):
        piece = column(g, t, at_x)
        send(piece, piece, cs.at[g, t], cr.at[g, t], device(x, 1 - c, z, y))

    def core_wait(g, t):
        wait(full[g].at[t, :, c], cr.at[g, t])

    def x_start(g, t):
        piece = column(g, t, x)
        send(piece, piece, xs.at[g, t], xr.at[g, t, 0], device(along_x(1), c, z, y))
        send(piece, piece, xs.at[g, t], xr.at[g, t, 1], device(along_x(-1), c, z, y))
        core_start(g, t, x)

    def x_relay(g, t):
        for side, (origin, onward) in enumerate(((-1, 1), (1, -1))):
            at_x = along_x(origin)
            wait(column(g, t, at_x), xr.at[g, t, side])
            piece = full[g].at[t, at_x, c, pl.ds(side * (NZ // 2), NZ // 2)]
            send(piece, piece, rs.at[g, t], rr.at[g, t], device(along_x(onward), c, z, y))
            core_start(g, t, at_x)

    def x_finish(g, t):
        at_x = along_x(2)
        wait(column(g, t, at_x), rr.at[g, t])
        core_start(g, t, at_x)

    def make_mask():
        lists_copy.wait()
        numbers = lax.broadcasted_iota(jnp.int32, (NZ, NZ), 0)
        for t in range(2):
            matches = (lists[t, pl.ds(z, 1), :] == numbers).astype(jnp.float32)
            total = jnp.sum(matches, axis=1, keepdims=True)
            mask[pl.ds(t * NZ, NZ), :] = jnp.broadcast_to(total, (NZ, BLK))

    def half_unit(t, k):
        p = wanted(z, k)
        for h in range(2):
            for n in range(NZ):
                block = occ[t, p, h, n].reshape(BLK, BLK)
                block = block * mask[pl.ds(t * NZ + n, 1), :]
                high, low = split(block)
                one_high[pl.ds(n * BLK, BLK), pl.ds(h * BLK, BLK)] = high
                one_low[pl.ds(n * BLK, BLK), pl.ds(h * BLK, BLK)] = low
        product = three_pass(int_high[...], int_low[...], one_high[...], one_low[...])
        for h in range(2):
            keep = mask[pl.ds(t * NZ + 2 * p + h, 1), :]
            for r in range(NY):
                part = product[r * BLK : (r + 1) * BLK, h * BLK : (h + 1) * BLK]
                sending[t, 2 * p + h, r] = part * keep
        for d in (2, 1, 3):
            to_y = along_y(d)
            for h in range(2):
                to_z = 2 * p + h
                send(
                    sending.at[t, to_z, to_y], received.at[t, z, y],
                    out_sem.at[t], in_sem.at[t, pair], device(x, c, to_z, to_y),
                )
        for h in range(2):
            to_z = 2 * p + h
            source, target = sending.at[t, to_z, y], received.at[t, z, y]

            @pl.when(to_z == z)
            def _():
                pltpu.make_async_copy(source, target, in_sem.at[t, pair]).start()

            @pl.when(to_z != z)
            def _():
                send(source, target, out_sem.at[t], in_sem.at[t, pair], device(x, c, to_z, y))

    def half_stage(t):
        def unit(k, carry):
            half_unit(t, k)
            return carry

        lax.fori_loop(0, NX, unit, 0)

    def full_stage(t):
        def unit(k, carry):
            p = lax.rem(pair + 2 - k + NX, NX)
            wait(received.at[t, pl.ds(2 * p, 2)], in_sem.at[t, p])
            for h in range(2):
                for q in range(NY):
                    high, low = split(received[t, 2 * p + h, q])
                    two_high[pl.ds(h * BLK, BLK), pl.ds(q * BLK, BLK)] = high
                    two_low[pl.ds(h * BLK, BLK), pl.ds(q * BLK, BLK)] = low

            def tile(s, inner):
                halves = [
                    split(vir[t, p, h, pl.ds(2 * s, 2)].reshape(2 * BLK, BLK))
                    for h in range(2)
                ]
                high = jnp.concatenate([halves[0][0], halves[1][0]], axis=1)
                low = jnp.concatenate([halves[0][1], halves[1][1]], axis=1)
                product = three_pass(high, low, two_high[...], two_low[...])
                for q in range(NY):
                    at = (t, q, pl.ds(s * 2 * BLK, 2 * BLK), slice(None))
                    coupled[at] += product[:, q * BLK : (q + 1) * BLK]
                return inner

            lax.fori_loop(0, NZ // 2, tile, 0)
            return carry

        lax.fori_loop(0, NX, unit, 0)

    first_x_start()
    z_start(OCC, 1)
    first_z_start()
    z_start(VIR, 0)
    z_start(VIR, 1)
    rows_copy.wait()
    for r in range(NY):
        high, low = split(rows[r])
        int_high[pl.ds(r * BLK, BLK), :] = high
        int_low[pl.ds(r * BLK, BLK), :] = low
    make_mask()
    coupled[...] = jnp.zeros_like(coupled)

    def first_unit(k):
        first_finish(k)
        half_unit(0, k)

    first_y_start(0)
    first_y_start(1)
    first_y_relay(0)
    first_y_start(2)
    first_y_relay(1)
    first_y_start(3)
    z_wait(OCC, 1)
    y_start(OCC, 1)
    first_unit(0)
    first_y_relay(2)
    first_unit(1)
    first_y_relay(3)
    y_wait(OCC, 1)
    x_start(OCC, 1)
    for t in range(2):
        z_wait(VIR, t)
        y_start(VIR, t)
    first_unit(2)
    first_unit(3)
    x_relay(OCC, 1)
    y_wait(VIR, 0)
    x_start(VIR, 0)
    x_finish(OCC, 1)
    core_wait(OCC, 1)
    half_stage(1)
    x_relay(VIR, 0)
    y_wait(VIR, 1)
    x_start(VIR, 1)
    x_finish(VIR, 0)
    core_wait(VIR, 0)
    x_relay(VIR, 1)
    x_finish(VIR, 1)
    core_wait(VIR, 1)
    full_stage(0)
    full_stage(1)

    wait(occ.at[0, pl.ds(0, NX - 1), c, z, y], x0s)
    wait(occ.at[0, :, c, pl.ds(0, NZ - 1), y], z0s)
    wait(occ.at[0, :, c, :, pl.ds(0, 2)], y0s)
    wait(occ.at[0, :, c, :, 0], r0s)
    wait(occ.at[0, :, c], c0s)
    for g, t in ((OCC, 1), (VIR, 0), (VIR, 1)):
        wait(full[g].at[t, x, c, pl.ds(0, NZ - 1), y], zs.at[g, t])
        wait(full[g].at[t, x, c, :, pl.ds(0, NY - 1)], ys.at[g, t])
        wait(full[g].at[t, pl.ds(0, 2), c], xs.at[g, t])
        wait(full[g].at[t, 0, c], rs.at[g, t])
        wait(full[g].at[t, :, c], cs.at[g, t])
    for t in range(2):
        wait(sending.at[t, pl.ds(0, NZ - 1)], out_sem.at[t])
        wait(sending.at[t, 0, pl.ds(0, NY - 1)], out_sem.at[t])


def local(three_center, tile_lists, occ_density, vir_density):
    times, blocks = tile_lists.shape[0], tile_lists.shape[3]
    orbitals = three_center.shape[3]
    dma = pltpu.SemaphoreType.DMA
    coupled = pl.pallas_call(
        kernel,
        out_shape=pltpu.VMEM((times, NY, orbitals, BLK), jnp.float32),
        in_specs=[pl.BlockSpec(memory_space=pltpu.HBM)] * 4,
        out_specs=pl.BlockSpec(memory_space=pltpu.VMEM),
        scratch_shapes=[
            pltpu.VMEM((times, blocks, blocks), jnp.int32),
            pltpu.VMEM((times * blocks, BLK), jnp.float32),
            pltpu.VMEM((NY, BLK, orbitals), jnp.float32),
            pltpu.VMEM((NY * BLK, orbitals), jnp.bfloat16),
            pltpu.VMEM((NY * BLK, orbitals), jnp.bfloat16),
            pltpu.VMEM((times, NX, NC, NZ, NY, 32, BLK), jnp.float32),
            pltpu.VMEM((times, NX, NC, NZ, NY, 32, BLK), jnp.float32),
            pltpu.VMEM((times, NZ, NY, BLK, BLK), jnp.float32),
            pltpu.VMEM((times, NZ, NY, BLK, BLK), jnp.float32),
            pltpu.VMEM((orbitals, 2 * BLK), jnp.bfloat16),
            pltpu.VMEM((orbitals, 2 * BLK), jnp.bfloat16),
            pltpu.VMEM((2 * BLK, NY * BLK), jnp.bfloat16),
            pltpu.VMEM((2 * BLK, NY * BLK), jnp.bfloat16),
            dma((2,)),
            dma((2, 2)),
            dma((2, 2)),
            dma((2, 2)),
            dma((2, 2)),
            dma((2, 2)),
            dma((2, 2)),
            dma((2, 2, 2)),
            dma((2, 2)),
            dma((2, 2)),
            dma((2, 2)),
            dma((2, 2)),
            dma((2,)),
            dma((2, NX)),
            dma(()),
            dma(()),
            dma(()),
            dma((NX,)),
            dma(()),
            dma((NX, 2)),
            dma(()),
            dma((NX,)),
            dma(()),
            dma((NX,)),
        ],
        compiler_params=pltpu.CompilerParams(
            collective_id=0, has_side_effects=True, vmem_limit_bytes=36 * 2**20
        ),
        name="contract",
    )(*(pltpu.with_memory_space_constraint(a, pltpu.HBM) for a in (tile_lists, three_center, occ_density, vir_density)))
    return coupled[:, :, None]


def solution(mesh):
    in_specs = (
        P("aux", "orb", None, None),
        P(None, "aux", None, None),
        P(None, "orb", "aux"),
        P(None, "orb", "aux"),
    )
    out_specs = P(None, "aux", "orb", None, None)
    return jax.shard_map(local, mesh=mesh, in_specs=in_specs, out_specs=out_specs, check_vma=False)
```

```python
import functools

import jax
import jax.numpy as jnp
from jax import lax
from jax.experimental import pallas as pl
from jax.experimental.pallas import tpu as pltpu
from jax.sharding import PartitionSpec as P

MESH = pl.DeviceIdType.MESH
NX, NC, NZ, NY = 4, 2, 8, 4
BLK = 128
OCC, VIR = 0, 1


def split(value):
    high = value.astype(jnp.bfloat16)
    return high, (value - high.astype(jnp.float32)).astype(jnp.bfloat16)


def three_pass(a_high, a_low, b_high, b_low):
    dot = functools.partial(jnp.dot, preferred_element_type=jnp.float32)
    return dot(a_high, b_high) + dot(a_high, b_low) + dot(a_low, b_high)


def kernel(
    tile_lists, three_center, occ_in, vir_in, coupled,
    lists, mask, rows, int_high, int_low, occ, vir, sending, received,
    one_high, one_low, two_high, two_low,
    rows_sem, own_sem, zs, zr, ys, yr, xs, xr, rs, rr, cs, cr, out_sem, in_sem,
    x0s, x0r, z0s, z0r, y0s, y0r, r0s, r0r, c0s, c0r,
):
    aux, orb = lax.axis_index("aux"), lax.axis_index("orb")
    x, c, z, y = lax.div(aux, NC), lax.rem(aux, NC), lax.div(orb, NY), lax.rem(orb, NY)
    pair = lax.div(z, 2)
    inputs, full = (occ_in, vir_in), (occ, vir)

    def device(at_x, at_c, at_z, at_y):
        return (at_x * NC + at_c, at_z * NY + at_y)

    def along_x(step):
        return lax.rem(x + step + NX, NX)

    def along_z(step):
        return lax.rem(z + step, NZ)

    def along_y(step):
        return lax.rem(y + step, NY)

    def send(source, target, send_sem, recv_sem, to):
        pltpu.make_async_remote_copy(
            src_ref=source, dst_ref=target, send_sem=send_sem, recv_sem=recv_sem,
            device_id=to, device_id_type=MESH,
        ).start()

    def wait(ref, sem):
        pltpu.make_async_copy(ref, ref, sem).wait()

    def own_copy(g, t):
        return pltpu.make_async_copy(inputs[g].at[t], full[g].at[t, x, c, z, y], own_sem.at[g, t])

    rows_copy = pltpu.make_async_copy(three_center.at[:, 0], rows, rows_sem.at[0])
    lists_copy = pltpu.make_async_copy(tile_lists.at[:, y], lists, rows_sem.at[1])
    for g in (OCC, VIR):
        for t in range(2):
            own_copy(g, t).start()
    lists_copy.start()
    rows_copy.start()

    barrier = pltpu.get_barrier_semaphore()
    peers = [device(x, c, along_z(d), y) for d in range(1, NZ)]
    peers += [device(x, c, z, along_y(d)) for d in range(1, NY)]
    peers += [device(along_x(d), c, z, y) for d in range(1, NX)]
    peers += [device(x, 1 - c, z, y)]
    for peer in peers:
        pl.semaphore_signal(barrier, inc=1, device_id=peer, device_id_type=MESH)
    pl.semaphore_wait(barrier, len(peers))

    def wanted(at_z, k):
        return lax.rem(lax.div(at_z, 2) + 2 + k, NX)

    def first_x_start():
        own_copy(OCC, 0).wait()
        piece = occ.at[0, x, c, z, y]
        for d in (2, 1, 3):
            send(piece, piece, x0s, x0r, device(along_x(d), c, z, y))

    def first_z_start():
        wait(occ.at[0, pl.ds(0, NX - 1), c, z, y], x0r)
        for k in range(NX):
            for d in (4, 3, 5, 2, 6, 1, 7):
                at_z = along_z(d)
                piece = occ.at[0, wanted(at_z, k), c, z, y]
                send(piece, piece, z0s, z0r.at[k], device(x, c, at_z, y))

    def first_y_start(k):
        wait(occ.at[0, 0, c, pl.ds(0, NZ - 1), y], z0r.at[k])
        piece = occ.at[0, wanted(z, k), c, :, y]
        for side, step in enumerate((1, 3)):
            send(piece, piece, y0s, y0r.at[k, side], device(x, c, z, along_y(step)))

    def first_y_relay(k):
        for side, (origin, onward) in enumerate(((3, 1), (1, 3))):
            from_y, to_y = along_y(origin), along_y(onward)
            wait(occ.at[0, 0, c, :, from_y], y0r.at[k, side])
            piece = occ.at[0, wanted(z, k), c, pl.ds(side * (NZ // 2), NZ // 2), from_y]
            send(piece, piece, r0s, r0r.at[k], device(x, c, z, to_y))

    def first_finish(k):
        wait(occ.at[0, 0, c, :, y], r0r.at[k])
        piece = occ.at[0, wanted(z, k), c]
        send(piece, piece, c0s, c0r.at[k], device(x, 1 - c, z, y))
        wait(piece, c0r.at[k])

    def z_start(g, t):
        own_copy(g, t).wait()
        piece = full[g].at[t, x, c, z, y]
        for d in (4, 3, 5, 2, 6, 1, 7):
            send(piece, piece, zs.at[g, t], zr.at[g, t], device(x, c, along_z(d), y))

    def z_wait(g, t):
        wait(full[g].at[t, x, c, pl.ds(0, NZ - 1), y], zr.at[g, t])

    def y_start(g, t):
        piece = full[g].at[t, x, c, :, y]
        for d in (2, 1, 3):
            send(piece, piece, ys.at[g, t], yr.at[g, t], device(x, c, z, along_y(d)))

    def y_wait(g, t):
        wait(full[g].at[t, x, c, :, pl.ds(0, NY - 1)], yr.at[g, t])

    def column(g, t, at_x):
        return full[g].at[t, at_x, c]

    def core_start(g, t, at_x):
        piece = column(g, t, at_x)
        send(piece, piece, cs.at[g, t], cr.at[g, t], device(x, 1 - c, z, y))

    def core_wait(g, t):
        wait(full[g].at[t, :, c], cr.at[g, t])

    def x_start(g, t):
        piece = column(g, t, x)
        send(piece, piece, xs.at[g, t], xr.at[g, t, 0], device(along_x(1), c, z, y))
        send(piece, piece, xs.at[g, t], xr.at[g, t, 1], device(along_x(-1), c, z, y))
        core_start(g, t, x)

    def x_relay(g, t):
        for side, (origin, onward) in enumerate(((-1, 1), (1, -1))):
            at_x = along_x(origin)
            wait(column(g, t, at_x), xr.at[g, t, side])
            piece = full[g].at[t, at_x, c, pl.ds(side * (NZ // 2), NZ // 2)]
            send(piece, piece, rs.at[g, t], rr.at[g, t], device(along_x(onward), c, z, y))
            core_start(g, t, at_x)

    def x_finish(g, t):
        at_x = along_x(2)
        wait(column(g, t, at_x), rr.at[g, t])
        core_start(g, t, at_x)

    def make_mask():
        lists_copy.wait()
        numbers = lax.broadcasted_iota(jnp.int32, (NZ, NZ), 0)
        for t in range(2):
            matches = (lists[t, pl.ds(z, 1), :] == numbers).astype(jnp.float32)
            total = jnp.sum(matches, axis=1, keepdims=True)
            mask[pl.ds(t * NZ, NZ), :] = jnp.broadcast_to(total, (NZ, BLK))

    def half_unit(t, k):
        p = wanted(z, k)
        for h in range(2):
            for n in range(NZ):
                block = occ[t, p, h, n].reshape(BLK, BLK)
                block = block * mask[pl.ds(t * NZ + n, 1), :]
                high, low = split(block)
                one_high[pl.ds(n * BLK, BLK), pl.ds(h * BLK, BLK)] = high
                one_low[pl.ds(n * BLK, BLK), pl.ds(h * BLK, BLK)] = low
        product = three_pass(int_high[...], int_low[...], one_high[...], one_low[...])
        for h in range(2):
            keep = mask[pl.ds(t * NZ + 2 * p + h, 1), :]
            for r in range(NY):
                part = product[r * BLK : (r + 1) * BLK, h * BLK : (h + 1) * BLK]
                sending[t, 2 * p + h, r] = part * keep
        for d in (2, 1, 3):
            to_y = along_y(d)
            for h in range(2):
                to_z = 2 * p + h
                send(
                    sending.at[t, to_z, to_y], received.at[t, z, y],
                    out_sem.at[t], in_sem.at[t, pair], device(x, c, to_z, to_y),
                )
        for h in range(2):
            to_z = 2 * p + h
            source, target = sending.at[t, to_z, y], received.at[t, z, y]

            @pl.when(to_z == z)
            def _():
                pltpu.make_async_copy(source, target, in_sem.at[t, pair]).start()

            @pl.when(to_z != z)
            def _():
                send(source, target, out_sem.at[t], in_sem.at[t, pair], device(x, c, to_z, y))

    def half_stage(t):
        def unit(k, carry):
            half_unit(t, k)
            return carry

        lax.fori_loop(0, NX, unit, 0)

    def full_stage(t):
        def unit(k, carry):
            p = lax.rem(pair + 2 - k + NX, NX)
            wait(received.at[t, pl.ds(2 * p, 2)], in_sem.at[t, p])
            for h in range(2):
                for q in range(NY):
                    high, low = split(received[t, 2 * p + h, q])
                    two_high[pl.ds(h * BLK, BLK), pl.ds(q * BLK, BLK)] = high
                    two_low[pl.ds(h * BLK, BLK), pl.ds(q * BLK, BLK)] = low

            def tile(s, inner):
                halves = [
                    split(vir[t, p, h, pl.ds(2 * s, 2)].reshape(2 * BLK, BLK))
                    for h in range(2)
                ]
                high = jnp.concatenate([halves[0][0], halves[1][0]], axis=1)
                low = jnp.concatenate([halves[0][1], halves[1][1]], axis=1)
                product = three_pass(high, low, two_high[...], two_low[...])
                for q in range(NY):
                    at = (t, q, pl.ds(s * 2 * BLK, 2 * BLK), slice(None))
                    coupled[at] += product[:, q * BLK : (q + 1) * BLK]
                return inner

            lax.fori_loop(0, NZ // 2, tile, 0)
            return carry

        lax.fori_loop(0, NX, unit, 0)

    first_x_start()
    z_start(OCC, 1)
    first_z_start()
    z_start(VIR, 0)
    z_start(VIR, 1)
    rows_copy.wait()
    for r in range(NY):
        high, low = split(rows[r])
        int_high[pl.ds(r * BLK, BLK), :] = high
        int_low[pl.ds(r * BLK, BLK), :] = low
    make_mask()
    coupled[...] = jnp.zeros_like(coupled)

    def first_unit(k):
        first_finish(k)
        half_unit(0, k)

    first_y_start(0)
    first_y_start(1)
    first_y_relay(0)
    first_y_start(2)
    first_y_relay(1)
    first_y_start(3)
    z_wait(OCC, 1)
    y_start(OCC, 1)
    first_unit(0)
    first_y_relay(2)
    first_unit(1)
    first_y_relay(3)
    y_wait(OCC, 1)
    x_start(OCC, 1)
    first_unit(2)
    first_unit(3)
    z_wait(VIR, 0)
    y_start(VIR, 0)
    z_wait(VIR, 1)
    y_start(VIR, 1)
    x_relay(OCC, 1)
    y_wait(VIR, 0)
    x_start(VIR, 0)
    x_finish(OCC, 1)
    core_wait(OCC, 1)
    half_stage(1)
    x_relay(VIR, 0)
    y_wait(VIR, 1)
    x_start(VIR, 1)
    x_finish(VIR, 0)
    core_wait(VIR, 0)
    x_relay(VIR, 1)
    x_finish(VIR, 1)
    core_wait(VIR, 1)
    full_stage(0)
    full_stage(1)

    wait(occ.at[0, pl.ds(0, NX - 1), c, z, y], x0s)
    wait(occ.at[0, :, c, pl.ds(0, NZ - 1), y], z0s)
    wait(occ.at[0, :, c, :, pl.ds(0, 2)], y0s)
    wait(occ.at[0, :, c, :, 0], r0s)
    wait(occ.at[0, :, c], c0s)
    for g, t in ((OCC, 1), (VIR, 0), (VIR, 1)):
        wait(full[g].at[t, x, c, pl.ds(0, NZ - 1), y], zs.at[g, t])
        wait(full[g].at[t, x, c, :, pl.ds(0, NY - 1)], ys.at[g, t])
        wait(full[g].at[t, pl.ds(0, 2), c], xs.at[g, t])
        wait(full[g].at[t, 0, c], rs.at[g, t])
        wait(full[g].at[t, :, c], cs.at[g, t])
    for t in range(2):
        wait(sending.at[t, pl.ds(0, NZ - 1)], out_sem.at[t])
        wait(sending.at[t, 0, pl.ds(0, NY - 1)], out_sem.at[t])


def local(three_center, tile_lists, occ_density, vir_density):
    times, blocks = tile_lists.shape[0], tile_lists.shape[3]
    orbitals = three_center.shape[3]
    dma = pltpu.SemaphoreType.DMA
    coupled = pl.pallas_call(
        kernel,
        out_shape=pltpu.VMEM((times, NY, orbitals, BLK), jnp.float32),
        in_specs=[pl.BlockSpec(memory_space=pltpu.HBM)] * 4,
        out_specs=pl.BlockSpec(memory_space=pltpu.VMEM),
        scratch_shapes=[
            pltpu.VMEM((times, blocks, blocks), jnp.int32),
            pltpu.VMEM((times * blocks, BLK), jnp.float32),
            pltpu.VMEM((NY, BLK, orbitals), jnp.float32),
            pltpu.VMEM((NY * BLK, orbitals), jnp.bfloat16),
            pltpu.VMEM((NY * BLK, orbitals), jnp.bfloat16),
            pltpu.VMEM((times, NX, NC, NZ, NY, 32, BLK), jnp.float32),
            pltpu.VMEM((times, NX, NC, NZ, NY, 32, BLK), jnp.float32),
            pltpu.VMEM((times, NZ, NY, BLK, BLK), jnp.float32),
            pltpu.VMEM((times, NZ, NY, BLK, BLK), jnp.float32),
            pltpu.VMEM((orbitals, 2 * BLK), jnp.bfloat16),
            pltpu.VMEM((orbitals, 2 * BLK), jnp.bfloat16),
            pltpu.VMEM((2 * BLK, NY * BLK), jnp.bfloat16),
            pltpu.VMEM((2 * BLK, NY * BLK), jnp.bfloat16),
            dma((2,)),
            dma((2, 2)),
            dma((2, 2)),
            dma((2, 2)),
            dma((2, 2)),
            dma((2, 2)),
            dma((2, 2)),
            dma((2, 2, 2)),
            dma((2, 2)),
            dma((2, 2)),
            dma((2, 2)),
            dma((2, 2)),
            dma((2,)),
            dma((2, NX)),
            dma(()),
            dma(()),
            dma(()),
            dma((NX,)),
            dma(()),
            dma((NX, 2)),
            dma(()),
            dma((NX,)),
            dma(()),
            dma((NX,)),
        ],
        compiler_params=pltpu.CompilerParams(
            collective_id=0, has_side_effects=True, vmem_limit_bytes=36 * 2**20
        ),
        name="contract",
    )(*(pltpu.with_memory_space_constraint(a, pltpu.HBM) for a in (tile_lists, three_center, occ_density, vir_density)))
    return coupled[:, :, None]


def solution(mesh):
    in_specs = (
        P("aux", "orb", None, None),
        P(None, "aux", None, None),
        P(None, "orb", "aux"),
        P(None, "orb", "aux"),
    )
    out_specs = P(None, "aux", "orb", None, None)
    return jax.shard_map(local, mesh=mesh, in_specs=in_specs, out_specs=out_specs, check_vma=False)
```
